32 devices in a mesh: fsdp: 2 (over x), ctx: 4 (over z), tp: 4 (over y, core).
Axes of the slice: x: 2, y: 2, z: 4, core: 2. Of those that a mesh axis runs over, the one named last changes fastest.
Arguments:
- layer_input: bfloat16 [2, 2048, 2048], P('fsdp', 'ctx'), may hold values from -6 to 6
- segment_ids: int32 [2, 2048], P('fsdp'), may hold values from 0 to 2, never falling along the last dimension, each value on 1 to 1536 neighbouring positions
- query_weight: bfloat16 [2048, 2048], P(('fsdp', 'ctx'), 'tp'), may hold values from -0.125 to 0.125
- key_weight: bfloat16 [2048, 2048], P(('fsdp', 'ctx'), 'tp'), may hold values from -0.125 to 0.125
- value_weight: bfloat16 [2048, 2048], P(('fsdp', 'ctx'), 'tp'), may hold values from -0.125 to 0.125
- output_weight: bfloat16 [2048, 2048], P(('fsdp', 'ctx'), 'tp'), may hold values from -2 to 2
- up_weight: bfloat16 [2048, 8192], P(('fsdp', 'ctx'), 'tp'), may hold values from -0.125 to 0.125
- down_weight: bfloat16 [2048, 8192], P(('fsdp', 'ctx'), 'tp'), may hold values from -0.0625 to 0.0625
- query_bias: float32 [2048], P('tp'), may hold values from -3 to 3
- value_bias: float32 [2048], P('tp'), may hold values from -3 to 3
- output_bias: float32 [2048], replicated, may hold values from -3 to 3
- up_bias: float32 [8192], P('tp'), may hold values from -3 to 3
- down_bias: float32 [2048], replicated, may hold values from -3 to 3
- first_gain: float32 [2048], replicated, may hold values from 0.1 to 1.9
- first_shift: float32 [2048], replicated, may hold values from -2 to 2
- second_gain: float32 [2048], replicated, may hold values from 0.1 to 1.9
- second_shift: float32 [2048], replicated, may hold values from -2 to 2
- cotangent: bfloat16 [2, 2048, 2048], P('fsdp', 'ctx'), may hold values from -6 to 6
Outputs:
- layer_output: bfloat16 [2, 2048, 2048], P('fsdp', 'ctx')
- input_gradient: float32 [2, 2048, 2048], P('fsdp', 'ctx')
- query_gradient: float32 [2048, 2048], P(('fsdp', 'ctx'), 'tp')
- key_gradient: float32 [2048, 2048], P(('fsdp', 'ctx'), 'tp')
- value_gradient: float32 [2048, 2048], P(('fsdp', 'ctx'), 'tp')
- output_gradient: float32 [2048, 2048], P(('fsdp', 'ctx'), 'tp')
- up_gradient: float32 [2048, 8192], P(('fsdp', 'ctx'), 'tp')
- down_gradient: float32 [2048, 8192], P(('fsdp', 'ctx'), 'tp')
- query_offset: float32 [2048], P('tp')
- value_offset: float32 [2048], P('tp')
- output_offset: float32 [2048], replicated
- up_offset: float32 [8192], P('tp')
- down_offset: float32 [2048], replicated
- first_scale: float32 [2048], replicated
- first_center: float32 [2048], replicated
- second_scale: float32 [2048], replicated
- second_center: float32 [2048], replicated
The draws below stay inside these ranges and needn't reach their ends.
Inputs may be any that keep to these rules, and one draw needn't show every extreme that they name: `segment_ids`: in each sequence the ids never fall and each of the 3 ids 0 to 2 appears; each document holds 1 to 1536 tokens, and one exactly 1536.
All inputs are finite; a program needn't handle non-finite values.
Results may differ from the reference program's by a relative error of at most 0.012.
Values may be sent and summed in bfloat16 or wider, within the bound.
No kernel may reach another device: no remote copies, remote signals or barrier semaphores. Data moves between devices by JAX's collectives and lax.ppermute only.
A program may use at most 256 MiB of HBM per device.

```python
import math
from functools import partial
import jax
import jax.numpy as jnp
import numpy as np
from jax import lax

D = 2048
HEADS = 16
HD = 128
FF = 8192
LEN = 2048
WINDOW = 1024
DOCS = 3
SEQS = 2
LONGEST = 1536


def levels(own_key, dims, pieces, least, top_value):
    factor_of, own = 1.0, jax.random.fold_in(own_key, 6)
    for dim, parts in pieces:
        draws = jnp.exp(jax.random.uniform(jax.random.fold_in(own, dim), (parts,), jnp.float32, least / len(pieces), top_value / len(pieces)))
        factor_of = factor_of * jnp.repeat(draws, dims[dim] // parts).reshape([-1 if axis == dim else 1 for axis in range(len(dims))])
    return factor_of


def split_up(count, total, reach, skew):
    portions = [(1 << 20) // math.isqrt(grade ** skew) + 1 for grade in range(2, count + 1)]
    spare, holding = total - reach - (count - 1), [1] * (count - 1)
    while spare > 0:
        candidates = [i for i in range(count - 1) if holding[i] < reach]
        mass, budget = sum([portions[i] for i in candidates]), spare
        for i in candidates:
            addition = min(reach - holding[i], max(1, budget * portions[i] // mass), spare)
            holding[i] = holding[i] + addition
            spare = spare - addition
    return np.array([reach] + holding)


def ragged(key, count, total, reach, slope):
    if count == 2:
        one = jax.random.randint(key, (), max(1, total - reach), min(reach, total - 1) + 1)
        return jnp.stack([one, total - one])
    sizes = jnp.asarray(split_up(count, total, reach, slope), jnp.int32)
    pairs = (count - 1) // 2
    giver, taker = sizes[1:1 + 2 * pairs:2], sizes[2:2 + 2 * pairs:2]
    slack = jnp.minimum(giver - 1, reach - taker)
    moved = jax.random.randint(jax.random.fold_in(key, 1), (pairs,), 0, 1 << 20) % (slack + 1)
    sizes = sizes.at[1:1 + 2 * pairs:2].set(giver - moved).at[2:2 + 2 * pairs:2].set(taker + moved)
    return sizes[jax.random.permutation(jax.random.fold_in(key, 2), count)]


def centred(rng, extent, deviation, most, shards=(), kind=jnp.bfloat16):
    array = deviation * jax.random.normal(rng, extent, jnp.float32)
    if shards:
        array = array * levels(rng, extent, shards, -0.22, 0.18)
    return jnp.clip(array, -most, most).astype(kind)


def setup_inputs(seed: int = 0) -> dict:
    key_of = jax.random.split(jax.random.key(seed), 19)
    return {
        "layer_input": centred(key_of[0], (SEQS, LEN, D), 1.0, 6.0, ((0, 2), (1, 4))),
        "segment_ids": jax.vmap(lambda own: jnp.searchsorted(jnp.cumsum(ragged(own, DOCS, LEN, LONGEST, 0)), jnp.arange(LEN), side="right"))(jax.random.split(key_of[1], SEQS)).reshape((SEQS, LEN)).astype(jnp.int32),
        "query_weight": centred(key_of[2], (D, D), D ** -0.5, 0.125, ((0, 8), (1, 4))),
        "key_weight": centred(key_of[3], (D, D), D ** -0.5, 0.125, ((0, 8), (1, 4))),
        "value_weight": centred(key_of[4], (D, D), D ** -0.5, 0.125, ((0, 8), (1, 4))),
        "output_weight": centred(key_of[5], (D, D), (max(D // 256, 1)) ** -0.5, 2.0, ((0, 8), (1, 4))),
        "up_weight": centred(key_of[6], (D, FF), D ** -0.5, 0.125, ((0, 8), (1, 4))),
        "down_weight": centred(key_of[7], (D, FF), FF ** -0.5, 0.0625, ((0, 8), (1, 4))),
        "query_bias": centred(key_of[8], (D,), 0.5, 3.0, ((0, 4),), jnp.float32),
        "value_bias": centred(key_of[9], (D,), 0.5, 3.0, ((0, 4),), jnp.float32),
        "output_bias": centred(key_of[10], (D,), 0.5, 3.0, (), jnp.float32),
        "up_bias": centred(key_of[11], (FF,), 0.5, 3.0, ((0, 4),), jnp.float32),
        "down_bias": centred(key_of[12], (D,), 0.5, 3.0, (), jnp.float32),
        "first_gain": jnp.clip(1.0 + 0.18 * jax.random.normal(key_of[13], (D,), jnp.float32), 0.1, 1.9),
        "first_shift": centred(key_of[14], (D,), 0.3, 2.0, (), jnp.float32),
        "second_gain": jnp.clip(1.0 + 0.18 * jax.random.normal(key_of[15], (D,), jnp.float32), 0.1, 1.9),
        "second_shift": centred(key_of[16], (D,), 0.3, 2.0, (), jnp.float32),
        "cotangent": centred(key_of[17], (SEQS, LEN, D), 1.0, 6.0, ((0, 2), (1, 4))),
    }


EPSILON = 1e-05
HIGHEST = lax.Precision.HIGHEST

@jax.custom_vjp
def low(v):
    return lax.optimization_barrier(v.astype(jnp.bfloat16)).astype(jnp.float32)

@jax.custom_vjp
def low_back(v):
    return v

def low_keep(v):
    return (low(v), None)

def low_pass(kept, grad):
    return (grad,)

def back_keep(v):
    return (v, None)

def back_low(kept, grad):
    return (low(grad),)
low.defvjp(low_keep, low_pass)
low_back.defvjp(back_keep, back_low)

def normalize(values, gain, shift):
    center = values - lax.optimization_barrier(jnp.mean(values, axis=-1, keepdims=True))
    spread = lax.optimization_barrier(jnp.mean(center * center, axis=-1, keepdims=True))
    return center * lax.rsqrt(spread + EPSILON) * gain + shift

def matmul(left, right):
    return jnp.dot(left, right, precision=HIGHEST)

def head_attend(allowed, operands):
    query_head, key_head, value_head = operands
    scores = low_back(jnp.dot(query_head, key_head.T, precision=HIGHEST) * HD ** (-0.5))
    scores = jnp.where(allowed, scores, -jnp.inf)
    probs = low(jax.nn.softmax(scores, axis=-1))
    return jnp.dot(probs, value_head, precision=HIGHEST)

def split_heads(matrix):
    return matrix.reshape(LEN, HEADS, HD).transpose(1, 0, 2)

def sequence_layer(weights, sequence, segments):
    query_weight, key_weight, value_weight, output_weight, up_weight, down_weight, query_bias, value_bias, output_bias, up_bias, down_bias, first_gain, first_shift, second_gain, second_shift = weights
    normed = low(normalize(sequence, first_gain, first_shift))
    queries = low_back(low(matmul(normed, query_weight) + query_bias))
    keys = low_back(low(matmul(normed, key_weight)))
    values = low_back(low(matmul(normed, value_weight) + value_bias))
    position = jnp.arange(LEN)
    allowed = (position[None, :] <= position[:, None]) & (position[:, None] - position[None, :] < WINDOW)
    allowed = allowed & (segments[:, None] == segments[None, :])
    mixed = lax.map(jax.checkpoint(partial(head_attend, allowed)), (split_heads(queries), split_heads(keys), split_heads(values)))
    mixed = low_back(low(mixed.transpose(1, 0, 2).reshape(LEN, D)))
    branch = low_back(jnp.dot(mixed, output_weight.T, precision=HIGHEST) + output_bias)
    middle = sequence + branch
    second = low(normalize(middle, second_gain, second_shift))
    before = low_back(matmul(second, up_weight) + up_bias)
    active = low(jax.nn.gelu(before, approximate=False))
    feed = low_back(jnp.dot(active, down_weight.T, precision=HIGHEST) + down_bias)
    return middle + feed

def forward(weights, inputs, segment_ids):

    def advance(carry, operands):
        sequence, segments = operands
        return (carry, jax.checkpoint(sequence_layer)(weights, sequence, segments))
    unused, outputs = lax.scan(advance, jnp.zeros((), jnp.float32), (inputs, segment_ids))
    return outputs

def reference(layer_input, segment_ids, query_weight, key_weight, value_weight, output_weight, up_weight, down_weight, query_bias, value_bias, output_bias, up_bias, down_bias, first_gain, first_shift, second_gain, second_shift, cotangent):
    weights = tuple((member.astype(jnp.float32) for member in (query_weight, key_weight, value_weight, output_weight, up_weight, down_weight, query_bias, value_bias, output_bias, up_bias, down_bias, first_gain, first_shift, second_gain, second_shift)))
    inputs = layer_input.astype(jnp.float32)

    def apply_layer(params, values):
        return forward(params, values, segment_ids)
    result, pullback = jax.vjp(apply_layer, weights, inputs)
    weight_grads, input_grad = pullback(cotangent.astype(jnp.float32))
    grad_query, grad_key, grad_value, grad_output, grad_up, grad_down, grad_qbias, grad_vbias, grad_obias, grad_ubias, grad_dbias, grad_gfirst, grad_sfirst, grad_gsecond, grad_ssecond = weight_grads
    return (result.astype(jnp.bfloat16), input_grad, grad_query, grad_key, grad_value, grad_output, grad_up, grad_down, grad_qbias, grad_vbias, grad_obias, grad_ubias, grad_dbias, grad_gfirst, grad_sfirst, grad_gsecond, grad_ssecond)
```

```python
import jax
import jax.numpy as jnp
from jax import lax
from jax.sharding import PartitionSpec as P

HD = 128
WINDOW = 1024
EPSILON = 1e-05
F32 = jnp.float32
BF16 = jnp.bfloat16


def dot(left, right, dims):
    return lax.dot_general(left, right, (dims, ((), ())), preferred_element_type=F32)


def dot_nn(left, right):
    return dot(left, right, ((1,), (0,)))


def dot_tn(left, right):
    return dot(left, right, ((0,), (0,)))


def dot_nt(left, right):
    return dot(left, right, ((1,), (1,)))


def swap(value, axis, bit):
    count = lax.axis_size(axis)
    return lax.ppermute(value, axis, [(source, source ^ bit) for source in range(count)])


def along(value, axis, steps):
    count = lax.axis_size(axis)
    pairs = [(s, s + steps) for s in range(count) if 0 <= s + steps < count]
    return lax.ppermute(value, axis, pairs)


def in_order(place, mine, other, axis=0):
    first = place == 0
    return jnp.concatenate(
        [jnp.where(first, mine, other), jnp.where(first, other, mine)], axis=axis
    )


def statistics(values):
    center = values - jnp.mean(values, axis=-1, keepdims=True)
    inverse = lax.rsqrt(jnp.mean(center * center, axis=-1, keepdims=True) + EPSILON)
    return center * inverse, inverse


def norm_back(grad, gain, unit, inverse):
    inner = grad * gain
    return inverse * (
        inner
        - jnp.mean(inner, axis=-1, keepdims=True)
        - unit * jnp.mean(inner * unit, axis=-1, keepdims=True)
    )


def gelu_exact(values):
    return jax.nn.gelu(values, approximate=False)


def score_block(queries, keys, live):
    block, heads = queries.shape[0], queries.shape[1] // HD
    span = keys.shape[0]
    scores = jnp.einsum(
        "qhd,khd->hqk",
        queries.reshape(block, heads, HD),
        keys.reshape(span, heads, HD),
        preferred_element_type=F32,
    )
    return jnp.where(live[None], scores * HD ** (-0.5), -jnp.inf)


def attend(queries, keys, values, live):
    block, local = queries.shape
    span, heads = keys.shape[0], local // HD
    scores = score_block(queries, keys, live)
    highest = jnp.max(scores, axis=-1, keepdims=True)
    expo = jnp.exp(scores - highest)
    totals = jnp.sum(expo, axis=-1, keepdims=True)
    weights = (expo / totals).astype(BF16)
    mixed = jnp.einsum(
        "hqk,khd->qhd", weights, values.reshape(span, heads, HD), preferred_element_type=F32
    )
    return mixed.reshape(block, local).astype(BF16), (highest + jnp.log(totals))[..., 0]


def attend_back(queries, keys, values, live, log_totals, mixed_grad):
    block, local = queries.shape
    span, heads = keys.shape[0], local // HD
    probs = jnp.exp(score_block(queries, keys, live) - log_totals[..., None])
    mixed_heads = mixed_grad.reshape(block, heads, HD)
    value_part = jnp.einsum(
        "hqk,qhd->khd", probs.astype(BF16), mixed_heads, preferred_element_type=F32
    )
    prob_grad = jnp.einsum(
        "qhd,khd->hqk", mixed_heads, values.reshape(span, heads, HD), preferred_element_type=F32
    )
    row_delta = jnp.sum(probs * prob_grad, axis=-1, keepdims=True)
    score_grad = (probs * (prob_grad - row_delta)).astype(BF16)
    scale = HD ** (-0.5)
    query_part = scale * jnp.einsum(
        "hqk,khd->qhd", score_grad, keys.reshape(span, heads, HD), preferred_element_type=F32
    )
    key_part = scale * jnp.einsum(
        "hqk,qhd->khd", score_grad, queries.reshape(block, heads, HD), preferred_element_type=F32
    )
    return (
        query_part.reshape(block, local).astype(BF16),
        key_part.reshape(span, local).astype(BF16),
        value_part.reshape(span, local).astype(BF16),
    )


def paired(
    layer_input,
    segment_ids,
    query_weight,
    key_weight,
    value_weight,
    output_weight,
    up_weight,
    down_weight,
    query_bias,
    value_bias,
    output_bias,
    up_bias,
    down_bias,
    first_gain,
    first_shift,
    second_gain,
    second_shift,
    cotangent,
):
    unused, block, width = layer_input.shape
    rows, local = query_weight.shape
    units = up_weight.shape[1]
    mine = units // 2
    half, quarter = block // 2, block // 4
    pieces = lax.axis_size("ctx")
    f, c, t = (lax.axis_index(name) for name in ("fsdp", "ctx", "tp"))
    core = t % 2
    inputs = layer_input[0]
    upstream = cotangent[0]

    def rowwise(value, start, size):
        return lax.dynamic_slice_in_dim(value, start, size, 0)

    def colwise(value, start, size):
        return lax.dynamic_slice_in_dim(value, start, size, 1)

    def grouped(value):
        parts = [
            value[:, (i * pieces + j) * rows : (i * pieces + j + 1) * rows]
            for j in range(pieces)
            for i in range(2)
        ]
        return jnp.concatenate(parts, axis=1)

    def ungrouped(value):
        parts = [
            value[:, (j * 2 + i) * rows : (j * 2 + i + 1) * rows]
            for i in range(2)
            for j in range(pieces)
        ]
        return jnp.concatenate(parts, axis=1)

    def whole_rows(shard):
        along_ctx = lax.all_gather(shard, "ctx", axis=0, tiled=True)
        return in_order(f, along_ctx, swap(along_ctx, "fsdp", 1))

    def half_units(shard):
        kept = colwise(shard, f * mine, mine)
        given = colwise(shard, (1 - f) * mine, mine)
        pair = in_order(f, kept, swap(given, "fsdp", 1))
        return lax.all_gather(pair, "ctx", axis=0, tiled=True)

    kv_full = whole_rows(jnp.concatenate([key_weight, value_weight], axis=1))
    qo_full = whole_rows(jnp.concatenate([query_weight, output_weight], axis=1))
    up_mine = half_units(up_weight)
    down_mine = half_units(down_weight)
    query_full, output_full = qo_full[:, :local], qo_full[:, local:]

    own_quarter = rowwise(inputs, t * quarter, quarter)
    back_one = along(own_quarter, "ctx", 1)
    back_two = along(back_one, "ctx", 1)
    behind = jnp.stack([back_two, back_one])
    behind_y = swap(behind, "tp", 2)
    low = t < 2
    column = jnp.stack(
        [jnp.where(low, behind, behind_y), jnp.where(low, behind_y, behind)], axis=1
    )
    other_column = swap(column, "tp", 1)
    first_core = core == 0
    prior = jnp.stack(
        [jnp.where(first_core, column, other_column), jnp.where(first_core, other_column, column)],
        axis=2,
    ).reshape(2 * block, width)
    reach = jnp.concatenate([prior, inputs], axis=0)
    unit_reach, inverse_reach = statistics(reach.astype(F32))
    normed_reach = (unit_reach * first_gain + first_shift).astype(BF16)
    normed = normed_reach[2 * block :]

    queries = (dot_nn(normed, query_full) + query_bias).astype(BF16)
    key_values = dot_nn(normed_reach, kv_full)
    keys = key_values[:, :local].astype(BF16)
    values = (key_values[:, local:] + value_bias).astype(BF16)

    padded = jnp.pad(segment_ids[0], (2 * block, 0), constant_values=-1)
    key_segments = lax.dynamic_slice_in_dim(padded, c * block, 3 * block, 0)
    query_segments = lax.dynamic_slice_in_dim(segment_ids[0], c * block, block, 0)
    query_place = jnp.arange(block)[:, None] + 2 * block
    key_place = jnp.arange(3 * block)[None, :]
    live = (key_place <= query_place) & (query_place - key_place < WINDOW)
    live = live & (key_segments[None, :] == query_segments[:, None])

    mixed, log_totals = attend(queries, keys, values, live)

    def own_half(partial):
        narrow = partial.astype(BF16)
        kept = rowwise(narrow, core * half, half)
        given = rowwise(narrow, (1 - core) * half, half)
        chip = (kept.astype(F32) + swap(given, "tp", 1).astype(F32)).astype(BF16)
        return chip.astype(F32) + swap(chip, "tp", 2).astype(F32)

    def own_half_of_pair(partial):
        narrow = partial.astype(BF16)
        kept, given = narrow[:block], narrow[block:]
        chip = (kept.astype(F32) + swap(given, "tp", 1).astype(F32)).astype(BF16)
        pair = (chip[:half].astype(F32) + swap(chip[half:], "fsdp", 1).astype(F32)).astype(BF16)
        return pair.astype(F32) + swap(pair, "tp", 2).astype(F32)

    inputs_half = rowwise(inputs, core * half, half).astype(F32)
    upstream_half = rowwise(upstream, core * half, half)
    upstream_rest = rowwise(upstream, (1 - core) * half, half)

    branch = own_half(dot_nt(mixed, output_full)) + output_bias
    middle = inputs_half + branch
    second_unit, second_inverse = statistics(middle)
    second_half = grouped((second_unit * second_gain + second_shift).astype(BF16))
    second_both = jnp.concatenate([second_half, swap(second_half, "fsdp", 1)], axis=0)
    second = jnp.concatenate([second_both, swap(second_both, "tp", 1)], axis=0)

    given_half = grouped(upstream_half)
    met_half = swap(given_half, "fsdp", 1)
    met_rest = swap(met_half, "tp", 1)
    gradient = jnp.concatenate([given_half, met_half, grouped(upstream_rest), met_rest], axis=0)

    my_bias = lax.dynamic_slice_in_dim(up_bias, f * mine, mine, 0)
    before = dot_nn(second, up_mine) + my_bias
    active = gelu_exact(before).astype(BF16)

    down_grad = dot_tn(gradient, active).astype(BF16)
    active_grad = dot_nn(gradient, down_mine)
    unused, gelu_back = jax.vjp(gelu_exact, before)
    before_grad = gelu_back(active_grad)[0].astype(BF16)
    second_grad = ungrouped(own_half_of_pair(dot_nt(before_grad, up_mine)))
    up_grad = dot_tn(second, before_grad).astype(BF16)
    up_sum = jnp.sum(before_grad.astype(F32), axis=0)

    feed = ungrouped(own_half_of_pair(dot_nt(active, down_mine))) + down_bias
    output_half = (middle + feed).astype(BF16)
    layer_output = in_order(core, output_half, swap(output_half, "tp", 1))[None]

    middle_grad = upstream_half.astype(F32) + norm_back(
        second_grad, second_gain, second_unit, second_inverse
    )
    second_gsum = jnp.sum(second_grad * second_unit, axis=0)
    second_ssum = jnp.sum(second_grad, axis=0)
    down_sum = jnp.sum(upstream_half.astype(F32), axis=0)
    branch_half = middle_grad.astype(BF16)
    output_sum = jnp.sum(branch_half.astype(F32), axis=0)
    branch_grad = in_order(core, branch_half, swap(branch_half, "tp", 1))
    output_grad = dot_tn(branch_grad, mixed)
    mixed_grad = dot_nn(branch_grad, output_full).astype(BF16)

    query_back, key_part, value_part = attend_back(
        queries, keys, values, live, log_totals, mixed_grad
    )
    kv_part = jnp.concatenate([key_part, value_part], axis=1)
    query_grad = dot_tn(normed, query_back)
    kv_grad = dot_tn(normed_reach, kv_part)
    query_sum = jnp.sum(query_back.astype(F32), axis=0)
    value_sum = jnp.sum(value_part.astype(F32), axis=0)

    kv_back = (
        kv_part[2 * block :].astype(F32)
        + along(kv_part[block : 2 * block], "ctx", -1).astype(F32)
        + along(kv_part[:block], "ctx", -2).astype(F32)
    ).astype(BF16)
    normed_terms = dot_nt(query_back, query_full) + dot_nt(kv_back, kv_full)
    normed_grad = own_half(normed_terms)
    unit = rowwise(unit_reach[2 * block :], core * half, half)
    inverse = rowwise(inverse_reach[2 * block :], core * half, half)
    input_half = middle_grad + norm_back(normed_grad, first_gain, unit, inverse)
    first_gsum = jnp.sum(normed_grad * unit, axis=0)
    first_ssum = jnp.sum(normed_grad, axis=0)
    input_gradient = in_order(core, input_half, swap(input_half, "tp", 1))[None]

    def own_rows(grad):
        reach_rows = pieces * rows
        kept = rowwise(grad, f * reach_rows, reach_rows)
        given = rowwise(grad, (1 - f) * reach_rows, reach_rows).astype(BF16)
        both = (kept + swap(given, "fsdp", 1).astype(F32)).astype(BF16)
        return lax.psum_scatter(both, "ctx", scatter_dimension=0, tiled=True).astype(F32)

    def own_rows_of_units(grad):
        both = lax.psum_scatter(grad, "ctx", scatter_dimension=0, tiled=True)
        kept = rowwise(both, f * rows, rows)
        given = rowwise(both, (1 - f) * rows, rows)
        return in_order(f, kept, swap(given, "fsdp", 1), axis=1).astype(F32)

    shard_d = own_rows_of_units(down_grad)
    shard_u = own_rows_of_units(up_grad)
    shard_o = own_rows(output_grad)
    shard_kv = own_rows(kv_grad)
    shard_q = own_rows(query_grad)

    halves = jnp.concatenate(
        [output_sum, down_sum, first_gsum, first_ssum, second_gsum, second_ssum]
    )
    halves = halves + swap(halves, "tp", 1)
    up_place = lax.dynamic_update_slice_in_dim(jnp.zeros((units,), F32), up_sum, f * mine, 0)
    sums = jnp.concatenate([halves, query_sum, value_sum, up_place])
    sums = sums + swap(sums, "fsdp", 1)
    for bit in (1, 2):
        sums = sums + swap(sums, "ctx", bit)
    wide = [sums[i * width : (i + 1) * width] for i in range(6)]
    rest = sums[6 * width :]
    return (
        layer_output,
        input_gradient,
        shard_q,
        shard_kv[:, :local],
        shard_kv[:, local:],
        shard_o,
        shard_u,
        shard_d,
        rest[:local],
        rest[local : 2 * local],
        wide[0],
        rest[2 * local :],
        wide[1],
        wide[2],
        wide[3],
        wide[4],
        wide[5],
    )


def from_behind(value, axis, steps):
    count = lax.axis_size(axis)
    leading, last = (max(0, -steps), min(count, count - steps))
    return lax.ppermute(value, axis, [(source, source + steps) for source in range(leading, last)])


def normalize(values, gain, shift):
    center = values - jnp.mean(values, axis=-1, keepdims=True)
    spread = jnp.mean(center * center, axis=-1, keepdims=True)
    return center * lax.rsqrt(spread + EPSILON) * gain + shift


def tp_total(values):
    return lax.psum(values, "tp")


def contract_rows(left, right):
    return lax.dot_general(
        left, right, (((0,), (0,)), ((), ())), preferred_element_type=jnp.float32
    )


def contract_cols(left, right):
    return lax.dot_general(
        left, right, (((1,), (1,)), ((), ())), preferred_element_type=jnp.float32
    )


def shards(
    layer_input,
    segment_ids,
    query_weight,
    key_weight,
    value_weight,
    output_weight,
    up_weight,
    down_weight,
    query_bias,
    value_bias,
    output_bias,
    up_bias,
    down_bias,
    first_gain,
    first_shift,
    second_gain,
    second_shift,
    cotangent,
):
    seqs, block, width = layer_input.shape
    rows = seqs * block
    query_full, key_full, value_full, output_full, up_full, down_full = (
        lax.all_gather(query_weight, ("fsdp", "ctx"), axis=0, tiled=True),
        lax.all_gather(key_weight, ("fsdp", "ctx"), axis=0, tiled=True),
        lax.all_gather(value_weight, ("fsdp", "ctx"), axis=0, tiled=True),
        lax.all_gather(output_weight, ("fsdp", "ctx"), axis=0, tiled=True),
        lax.all_gather(up_weight, ("fsdp", "ctx"), axis=0, tiled=True),
        lax.all_gather(down_weight, ("fsdp", "ctx"), axis=0, tiled=True),
    )
    local = query_full.shape[1]
    heads = local // HD
    scale = HD ** (-0.5)
    inputs = layer_input.reshape(rows, width).astype(jnp.float32)
    upstream = cotangent.reshape(rows, width)
    normed = normalize(inputs, first_gain, first_shift).astype(jnp.bfloat16)
    queries = (jnp.dot(normed, query_full, preferred_element_type=jnp.float32) + query_bias).astype(
        jnp.bfloat16
    )
    keys = jnp.dot(normed, key_full, preferred_element_type=jnp.float32).astype(jnp.bfloat16)
    values = (jnp.dot(normed, value_full, preferred_element_type=jnp.float32) + value_bias).astype(
        jnp.bfloat16
    )
    query_blocks = queries.reshape(seqs, block, local)
    own_pair = jnp.stack([keys.reshape(seqs, block, local), values.reshape(seqs, block, local)])
    priors = []
    for distance in (1, 2):
        priors.append(from_behind(own_pair, "ctx", distance))
    key_pairs = jnp.concatenate([priors[1], priors[0], own_pair], axis=2)
    ctx_index = lax.axis_index("ctx")
    padded = jnp.pad(segment_ids, ((0, 0), (2 * block, 0)), constant_values=-1)
    key_segments = lax.dynamic_slice_in_dim(padded, ctx_index * block, 3 * block, 1)
    query_segments = lax.dynamic_slice_in_dim(segment_ids, ctx_index * block, block, 1)
    query_place = jnp.arange(block)[:, None] + 2 * block
    key_place = jnp.arange(3 * block)[None, :]
    window_mask = (key_place <= query_place) & (query_place - key_place < WINDOW)
    allowed = window_mask[None] & (key_segments[:, None, :] == query_segments[:, :, None])

    def score_block(query_seq, key_seq, live):
        scores = (
            jnp.einsum(
                "qhd,khd->hqk",
                query_seq.reshape(block, heads, HD),
                key_seq.reshape(3 * block, heads, HD),
                preferred_element_type=jnp.float32,
            )
            * scale
        )
        return jnp.where(live[None], scores, -jnp.inf)

    def attend(operands):
        query_seq, key_seq, value_seq, live = operands
        scores = score_block(query_seq, key_seq, live)
        highest = jnp.max(scores, axis=-1, keepdims=True)
        expo = jnp.exp(scores - highest)
        totals = jnp.sum(expo, axis=-1, keepdims=True)
        weights = (expo / totals).astype(jnp.bfloat16)
        mixed_seq = jnp.einsum(
            "hqk,khd->qhd",
            weights,
            value_seq.reshape(3 * block, heads, HD),
            preferred_element_type=jnp.float32,
        )
        return (
            mixed_seq.reshape(block, local).astype(jnp.bfloat16),
            (highest + jnp.log(totals))[..., 0],
        )

    mixed_blocks, log_totals = lax.map(attend, (query_blocks, key_pairs[0], key_pairs[1], allowed))
    mixed = mixed_blocks.reshape(rows, local)
    branch = tp_total(contract_cols(mixed, output_full)) + output_bias
    middle = inputs + branch
    second = normalize(middle, second_gain, second_shift).astype(jnp.bfloat16)
    before = jnp.dot(second, up_full, preferred_element_type=jnp.float32) + up_bias
    active = gelu_exact(before).astype(jnp.bfloat16)
    feed = tp_total(contract_cols(active, down_full)) + down_bias
    layer_output = (middle + feed).astype(jnp.bfloat16).reshape(seqs, block, width)
    upstream_wide = upstream.astype(jnp.float32)
    down_grad = contract_rows(upstream, active)
    down_sum = jnp.sum(upstream_wide, axis=0)
    active_grad = jnp.dot(upstream, down_full, preferred_element_type=jnp.float32)
    unused, gelu_back = jax.vjp(gelu_exact, before)
    before_grad = gelu_back(active_grad)[0].astype(jnp.bfloat16)
    up_grad = contract_rows(second, before_grad)
    up_sum = jnp.sum(before_grad.astype(jnp.float32), axis=0)
    second_grad = tp_total(contract_cols(before_grad, up_full))
    unused, second_back = jax.vjp(normalize, middle, second_gain, second_shift)
    middle_piece, second_gsum, second_ssum = second_back(second_grad)
    middle_grad = upstream_wide + middle_piece
    branch_grad = middle_grad.astype(jnp.bfloat16)
    output_grad = contract_rows(branch_grad, mixed)
    output_sum = jnp.sum(branch_grad.astype(jnp.float32), axis=0)
    mixed_grad = jnp.dot(branch_grad, output_full, preferred_element_type=jnp.float32).astype(
        jnp.bfloat16
    )

    def attend_back(operands):
        query_seq, key_seq, value_seq, live, log_seq, mixed_seq = operands
        scores = score_block(query_seq, key_seq, live)
        probs = jnp.exp(scores - log_seq[..., None])
        narrow = probs.astype(jnp.bfloat16)
        mixed_heads = mixed_seq.reshape(block, heads, HD)
        value_part = jnp.einsum(
            "hqk,qhd->khd", narrow, mixed_heads, preferred_element_type=jnp.float32
        )
        prob_grad = jnp.einsum(
            "qhd,khd->hqk",
            mixed_heads,
            value_seq.reshape(3 * block, heads, HD),
            preferred_element_type=jnp.float32,
        )
        row_delta = jnp.sum(probs * prob_grad, axis=-1, keepdims=True)
        score_grad = (probs * (prob_grad - row_delta)).astype(jnp.bfloat16)
        query_part = (
            jnp.einsum(
                "hqk,khd->qhd",
                score_grad,
                key_seq.reshape(3 * block, heads, HD),
                preferred_element_type=jnp.float32,
            )
            * scale
        )
        key_part = (
            jnp.einsum(
                "hqk,qhd->khd",
                score_grad,
                query_seq.reshape(block, heads, HD),
                preferred_element_type=jnp.float32,
            )
            * scale
        )
        return (
            query_part.reshape(block, local),
            key_part.reshape(3 * block, local),
            value_part.reshape(3 * block, local),
        )

    query_parts, key_parts, value_parts = lax.map(
        attend_back,
        (
            query_blocks,
            key_pairs[0],
            key_pairs[1],
            allowed,
            log_totals,
            mixed_grad.reshape(seqs, block, local),
        ),
    )
    pair_grads = jnp.stack([key_parts, value_parts])
    pair_total = pair_grads[:, :, 2 * block :]
    for distance in (1, 2):
        offset = (2 - distance) * block
        pair_total = pair_total + from_behind(
            pair_grads[:, :, offset : offset + block], "ctx", -distance
        )
    query_back = query_parts.reshape(rows, local).astype(jnp.bfloat16)
    key_back = pair_total[0].reshape(rows, local).astype(jnp.bfloat16)
    value_back = pair_total[1].reshape(rows, local).astype(jnp.bfloat16)
    query_grad = contract_rows(normed, query_back)
    key_grad = contract_rows(normed, key_back)
    value_grad = contract_rows(normed, value_back)
    query_sum = jnp.sum(query_back.astype(jnp.float32), axis=0)
    value_sum = jnp.sum(value_back.astype(jnp.float32), axis=0)
    normed_terms = (
        contract_cols(query_back, query_full)
        + contract_cols(key_back, key_full)
        + contract_cols(value_back, value_full)
    )
    normed_grad = tp_total(normed_terms)
    unused, first_back = jax.vjp(normalize, inputs, first_gain, first_shift)
    input_piece, first_gsum, first_ssum = first_back(normed_grad)
    input_gradient = (middle_grad + input_piece).reshape(seqs, block, width)
    shard_q, shard_k, shard_v, shard_o, shard_u, shard_d = (
        lax.psum_scatter(query_grad, ("fsdp", "ctx"), scatter_dimension=0, tiled=True),
        lax.psum_scatter(key_grad, ("fsdp", "ctx"), scatter_dimension=0, tiled=True),
        lax.psum_scatter(value_grad, ("fsdp", "ctx"), scatter_dimension=0, tiled=True),
        lax.psum_scatter(output_grad, ("fsdp", "ctx"), scatter_dimension=0, tiled=True),
        lax.psum_scatter(up_grad, ("fsdp", "ctx"), scatter_dimension=0, tiled=True),
        lax.psum_scatter(down_grad, ("fsdp", "ctx"), scatter_dimension=0, tiled=True),
    )
    (
        query_offset,
        value_offset,
        output_offset,
        up_offset,
        down_offset,
        first_scale,
        first_center,
        second_scale,
        second_center,
    ) = lax.psum(
        (
            query_sum,
            value_sum,
            output_sum,
            up_sum,
            down_sum,
            first_gsum,
            first_ssum,
            second_gsum,
            second_ssum,
        ),
        ("fsdp", "ctx"),
    )
    return (
        layer_output,
        input_gradient,
        shard_q,
        shard_k,
        shard_v,
        shard_o,
        shard_u,
        shard_d,
        query_offset,
        value_offset,
        output_offset,
        up_offset,
        down_offset,
        first_scale,
        first_center,
        second_scale,
        second_center,
    )


def solution(mesh):
    in_specs = (
        P("fsdp", "ctx", None),
        P("fsdp", None),
        P(("fsdp", "ctx"), "tp"),
        P(("fsdp", "ctx"), "tp"),
        P(("fsdp", "ctx"), "tp"),
        P(("fsdp", "ctx"), "tp"),
        P(("fsdp", "ctx"), "tp"),
        P(("fsdp", "ctx"), "tp"),
        P("tp"),
        P("tp"),
        P(),
        P("tp"),
        P(),
        P(),
        P(),
        P(),
        P(),
        P("fsdp", "ctx", None),
    )
    out_specs = (
        P("fsdp", "ctx", None),
        P("fsdp", "ctx", None),
        P(("fsdp", "ctx"), "tp"),
        P(("fsdp", "ctx"), "tp"),
        P(("fsdp", "ctx"), "tp"),
        P(("fsdp", "ctx"), "tp"),
        P(("fsdp", "ctx"), "tp"),
        P(("fsdp", "ctx"), "tp"),
        P("tp"),
        P("tp"),
        P(),
        P("tp"),
        P(),
        P(),
        P(),
        P(),
        P(),
    )
    sizes = dict(mesh.shape)
    fits = sizes == {"fsdp": 2, "ctx": 4, "tp": 4}
    body = paired if fits else shards
    return jax.shard_map(body, mesh=mesh, in_specs=in_specs, out_specs=out_specs, check_vma=False)
```
